32 devices in a mesh: gx: 4 (over y, core), gy: 4 (over z), gz: 2 (over x).
Axes of the slice: x: 2, y: 2, z: 4, core: 2. Of those that a mesh axis runs over, the one named last changes fastest.
Arguments:
- heat_source: float32 [64, 512, 512], P('gz', 'gx', 'gy'), may hold values from -18 to 18
- conductance: float32 [64, 512, 512], P('gz', 'gx', 'gy'), may hold values from 0.5 to 4
- projection: float32 [2, 4, 4, 3, 128, 128], P('gz', 'gx', 'gy'), may hold values from -1 to 2, as said below
- segment_map: int32 [2, 4, 4, 3, 128], P('gz', 'gx', 'gy'), may hold values from 0 to 127, each once within a row
Outputs:
- thermal_state: float32 [64, 512, 512], P('gz', 'gx', 'gy')
- multiplier_x: float32 [2, 4, 4, 32, 128], P('gz', 'gx', 'gy')
- multiplier_y: float32 [2, 4, 4, 32, 128], P('gz', 'gx', 'gy')
- multiplier_z: float32 [2, 4, 4, 128, 128], P('gz', 'gx', 'gy')
The draws below stay inside these ranges and needn't reach their ends.
Inputs may be any that keep to these rules, and one draw needn't show every extreme that they name: projection entries are finite.
All inputs are finite; a program needn't handle non-finite values.
Results may differ from the reference program's by a relative error of at most 0.0001.
Values sent between devices are 32-bit elements; how exact they have to be, the bound alone decides.
A program may use at most 128 MiB of HBM per device.

```python
import math
import jax
import jax.numpy as jnp
from jax import lax

C = 128
CZ = 32
ITERS = 4
SWEEPS = 2
NX = 512
NY = 512
NZ = 64
N_GX = 4
N_GY = 4
N_GZ = 2


def draw_projection(key, part):
    lattice_dimensions = (N_GZ, N_GX, N_GY, 3, C, C)
    spread = 0.5 / jnp.sqrt(jnp.float32(C))
    noise = jax.random.normal(key, lattice_dimensions, jnp.float32) * spread
    noise = jnp.clip(noise, -4.0 * spread, 4.0 * spread)
    return jnp.eye(C, dtype=jnp.float32) + noise


def level_of(key, dims, shards, low, top_value):
    loudness = 1.0
    for position, blocks in shards:
        draws = jax.random.uniform(jax.random.fold_in(jax.random.fold_in(key, 6), position), (blocks,), jnp.float32, low / len(shards), top_value / len(shards))
        loudness = loudness * jnp.repeat(jnp.exp(draws), dims[position] // blocks).reshape((-1,) + (1,) * (len(dims) - 1 - position))
    return loudness


def bell_draw(stream_key, shape, scale, bound, cuts=(), kind=jnp.bfloat16):
    factor_of = level_of(stream_key, shape, cuts, -0.22, 0.18) if cuts else 1.0
    drawn = jax.random.normal(stream_key, shape, jnp.float32) * scale * factor_of
    return jnp.minimum(jnp.maximum(drawn, -bound), bound).astype(kind)


def setup_inputs(seed: int = 0) -> dict:
    streams_of = jax.random.split(jax.random.key(seed), 5)
    return {
        "heat_source": bell_draw(streams_of[0], (NZ, NX, NY), 3.0, 18.0, ((0, 2), (1, 4), (2, 4)), jnp.float32),
        "conductance": jnp.clip(jnp.exp(math.log(4.0) - 2.0794415 * jax.random.uniform(streams_of[1], (NZ, NX, NY), jnp.float32) ** level_of(streams_of[1], (NZ, NX, NY), ((0, 2), (1, 4), (2, 4)), -0.2, 0.2)), 0.5, 4.0),
        "projection": draw_projection(jax.random.fold_in(streams_of[4], 71), 0),
        "segment_map": jax.vmap(lambda own: jax.random.permutation(own, C))(jax.random.split(streams_of[3], N_GZ * N_GX * N_GY * 3)).reshape((N_GZ, N_GX, N_GY, 3, C)).astype(jnp.int32),
    }


HIGH = lax.Precision.HIGHEST
DAMPING_WEIGHT = 0.8
EPSILON = 1e-6


def to_patches(field):
    return field.reshape(N_GZ, CZ, N_GX, C, N_GY, C).transpose(0, 2, 4, 1, 3, 5)


def collect_block_traces(blocks):
    return blocks.transpose(0, 3, 1, 4, 2, 5).reshape(N_GZ * CZ, N_GX * C, N_GY * C)


def laplacian_operate(field, main_coefficients):
    padded = jnp.pad(field, ((0, 0), (0, 0), (0, 0), (1, 1), (1, 1), (1, 1)))
    nearby = padded[..., 2:, 1:-1, 1:-1] + padded[..., :-2, 1:-1, 1:-1]
    nearby = nearby + padded[..., 1:-1, 2:, 1:-1] + padded[..., 1:-1, :-2, 1:-1]
    nearby = nearby + padded[..., 1:-1, 1:-1, 2:] + padded[..., 1:-1, 1:-1, :-2]
    return main_coefficients * field - nearby


def mortar(projection, segment_map):
    width = projection.shape[-1]
    onehot = (segment_map[..., :, None] == jnp.arange(width, dtype=jnp.int32)).astype(jnp.float32)
    return jnp.einsum("...se,...rs->...er", onehot, projection, precision=HIGH)


FACES = ((0, 1, "x"), (1, 2, "y"), (2, 0, "z"))


def coupling_mismatch_amounts(field, coupling_bases):
    uppers = (field[..., :, -1, :], field[..., :, :, -1], field[..., -1, :, :])
    firsts = (field[..., :, 0, :], field[..., :, :, 0], field[..., 0, :, :])
    counts = (N_GX, N_GY, N_GZ)
    result = []
    for face, patch_axis, label in FACES:
        beyond = jnp.roll(firsts[face], -1, axis=patch_axis)
        projected = jnp.einsum("...ke,...er->...kr", beyond, coupling_bases[..., face, :, :], precision=HIGH)
        count = counts[face]
        lattice_dimensions = [1, 1, 1, 1, 1]
        lattice_dimensions[patch_axis] = count
        final = (jnp.arange(count) == count - 1).reshape(lattice_dimensions)
        result.append(jnp.where(final, jnp.float32(0.0), uppers[face] - projected))
    return result


def lift_faces(mismatch_arrays, coupling_bases, lattice_dimensions):
    backs = []
    for face, patch_axis, label in FACES:
        back = -jnp.einsum("...kr,...er->...ke", mismatch_arrays[face], coupling_bases[..., face, :, :], precision=HIGH)
        backs.append(jnp.roll(back, 1, axis=patch_axis))
    total = jnp.zeros(lattice_dimensions, jnp.float32)
    total = total.at[..., :, -1, :].add(mismatch_arrays[0]).at[..., :, 0, :].add(backs[0])
    total = total.at[..., :, :, -1].add(mismatch_arrays[1]).at[..., :, :, 0].add(backs[1])
    total = total.at[..., -1, :, :].add(mismatch_arrays[2]).at[..., 0, :, :].add(backs[2])
    return total


def reference(heat_source, conductance, projection, segment_map):
    source = to_patches(heat_source)
    main_coefficients = 6.0 + to_patches(conductance)
    coupling_bases = mortar(projection, segment_map)
    lattice_dimensions = source.shape
    thermal_state = jnp.zeros(lattice_dimensions, jnp.float32)
    dual_flux_variables = [jnp.zeros(lattice_dimensions[:3] + (CZ, C), jnp.float32), jnp.zeros(lattice_dimensions[:3] + (CZ, C), jnp.float32), jnp.zeros(lattice_dimensions[:3] + (C, C), jnp.float32)]
    for iteration in range(ITERS):
        volumetric_supply = source - lift_faces(dual_flux_variables, coupling_bases, lattice_dimensions)
        for sweep_index in range(SWEEPS):
            thermal_state = thermal_state + DAMPING_WEIGHT * (volumetric_supply - laplacian_operate(thermal_state, main_coefficients)) / main_coefficients
        mismatch_arrays = coupling_mismatch_amounts(thermal_state, coupling_bases)
        lifted = lift_faces(mismatch_arrays, coupling_bases, lattice_dimensions)
        squares = sum(jnp.sum(jump * jump) for jump in mismatch_arrays)
        energy = jnp.sum(lifted * lifted / main_coefficients)
        alpha = squares / (energy + EPSILON)
        dual_flux_variables = [dual_flux_variables[face] + alpha * mismatch_arrays[face] for face in range(3)]
    return collect_block_traces(thermal_state), dual_flux_variables[0], dual_flux_variables[1], dual_flux_variables[2]
```

```python
import functools

import jax
import jax.numpy as jnp
from jax import lax
from jax.experimental import pallas as pl
from jax.experimental.pallas import tpu as pltpu
from jax.sharding import PartitionSpec as P

ITERS = 4
SWEEPS = 2
DAMPING_WEIGHT = 0.8
EPSILON = 1e-06
AXES = ("gx", "gy", "gz")
F32 = jnp.float32
BF16 = jnp.bfloat16
MESH = pl.DeviceIdType.MESH
NN = (((1,), (0,)), ((), ()))
NT = (((1,), (1,)), ((), ()))


def split(a):
    high = a.astype(BF16)
    return high, (a - high.astype(F32)).astype(BF16)


def dot3(a, high, low, dims):
    ah, al = split(a)
    mul = functools.partial(lax.dot_general, dimension_numbers=dims, preferred_element_type=F32)
    return mul(ah, high) + (mul(ah, low) + mul(al, high))


def tiles(a):
    return a.reshape(-1, 8, a.shape[-1]).sum(0)


def kernel(sizes, depth, width, heat, cond, proj, seg, out, mx, my, mz,
           f, p, va, vb, lifted, line, cols, layer, near_next, near_prev, znext, zprev,
           own, prev, high, low, jx, jy, jz, bx, by, bz, row, total,
           load_sem, store_sem, face_send, face_recv, mortar_send, mortar_recv, sum_send, sum_recv):
    n = sizes[0] * sizes[1] * sizes[2]
    me = [lax.axis_index(a) for a in AXES]
    rank = (me[0] * sizes[1] + me[1]) * sizes[2] + me[2]
    has_next = [me[d] < sizes[d] - 1 for d in range(3)]
    has_prev = [me[d] > 0 for d in range(3)]

    def peer(j):
        t = lax.rem(rank + j, n)
        return (t // (sizes[1] * sizes[2]), lax.rem(t // sizes[2], sizes[1]), lax.rem(t, sizes[2]))

    chunks = 4
    step = depth // chunks
    loads = []
    for c in range(chunks):
        part = pl.ds(c * step, step)
        for i, (src, dst) in enumerate(((heat, f), (cond, p))):
            copy = pltpu.make_async_copy(src.at[part], dst.at[part], load_sem.at[2 * c + i])
            copy.start()
            loads.append(copy)

    barrier = pltpu.get_barrier_semaphore()

    def greet(j, carry):
        pl.semaphore_signal(barrier, inc=1, device_id=peer(j), device_id_type=MESH)
        return carry

    lax.fori_loop(1, n, greet, 0)

    rows = lax.broadcasted_iota(jnp.int32, (width, width), 0)
    lanes = lax.broadcasted_iota(jnp.int32, (width, width), 1)
    for d in range(3):
        pick = jnp.where(seg[pl.ds(d, 1), :] == rows, F32(1), F32(0)).astype(BF16)
        ph, plow = split(proj[d])
        mh = lax.dot_general(pick, ph, NT, preferred_element_type=F32)
        ml = lax.dot_general(pick, plow, NT, preferred_element_type=F32)
        own[d] = mh + ml
        high[d] = mh.astype(BF16)
        low[d] = ml.astype(BF16)

    zero = jnp.zeros((width, width), F32)
    for v in (va, vb):
        v[0] = zero
        v[depth + 1] = zero
    cols[...] = zero

    for d in range(3):
        @pl.when(jnp.logical_not(has_next[d]))
        def _():
            if d < 2:
                near_next[d] = jnp.zeros((depth, width), F32)
            else:
                znext[...] = zero

        @pl.when(jnp.logical_not(has_prev[d]))
        def _():
            prev[d] = zero
            if d < 2:
                near_prev[d] = jnp.zeros((depth, width), F32)
            else:
                zprev[...] = zero

    pl.semaphore_wait(barrier, n - 1)

    def mortar_copy(d):
        return pltpu.make_async_remote_copy(
            src_ref=own.at[d], dst_ref=prev.at[d], send_sem=mortar_send.at[d], recv_sem=mortar_recv.at[d],
            device_id={AXES[d]: me[d] + 1}, device_id_type=MESH)

    for d in range(3):
        @pl.when(has_next[d])
        def _():
            mortar_copy(d).start()

    row8 = lax.broadcasted_iota(jnp.int32, (8, width), 0)
    first_lane = lanes == 0
    last_lane = lanes == width - 1

    def shift_rows(c):
        up = pltpu.roll(c, 1, 0)
        up = jnp.concatenate([jnp.where(row8 == 0, F32(0), up[:8]), up[8:]], 0)
        down = pltpu.roll(c, width - 1, 0)
        down = jnp.concatenate([down[:-8], jnp.where(row8 == 7, F32(0), down[-8:])], 0)
        return up + down

    def shift_lanes(c):
        return (jnp.where(first_lane, F32(0), pltpu.roll(c, 1, 1))
                + jnp.where(last_lane, F32(0), pltpu.roll(c, width - 1, 1)))

    def relax(v, z, supply, scale):
        c = v[z + 1]
        nearby = (v[z] + v[z + 2]) + shift_rows(c) + shift_lanes(c)
        return (1 - DAMPING_WEIGHT) * c + scale * (supply + nearby)

    def gather_faces(o, z):
        layer[0, pl.ds(z, 1), :] = o[0:1]
        layer[1, pl.ds(z, 1), :] = o[width - 1:width]
        cols[...] = jnp.where(lanes // 2 == z, pltpu.roll(o, 2 * z + 1, 1), cols[...])

    def close_faces():
        line[...] = cols[...].T
        layer[2] = line[pl.ds(1, depth, stride=2), :]
        layer[3] = line[pl.ds(0, depth, stride=2), :]

    for c in range(chunks):
        loads[2 * c].wait()
        loads[2 * c + 1].wait()

        def begin(z, carry):
            scale = DAMPING_WEIGHT / (6.0 + p[z])
            p[z] = scale
            vb[z + 1] = scale * f[z]
            return carry

        lax.fori_loop(c * step, (c + 1) * step, begin, 0)

    def face_copies(d):
        if d < 2:
            first, last, to_prev, to_next = layer.at[2 * d], layer.at[2 * d + 1], near_next.at[d], near_prev.at[d]
        else:
            first, last, to_prev, to_next = va.at[1], va.at[depth], znext, zprev
        back = pltpu.make_async_remote_copy(
            src_ref=first, dst_ref=to_prev, send_sem=face_send.at[2 * d], recv_sem=face_recv.at[2 * d],
            device_id={AXES[d]: me[d] - 1}, device_id_type=MESH)
        ahead = pltpu.make_async_remote_copy(
            src_ref=last, dst_ref=to_next, send_sem=face_send.at[2 * d + 1], recv_sem=face_recv.at[2 * d + 1],
            device_id={AXES[d]: me[d] + 1}, device_id_type=MESH)
        return back, ahead

    store = pltpu.make_async_copy(va.at[pl.ds(1, depth)], out, store_sem)
    jumps = (jx, jy, jz)
    backs = (bx, by, bz)
    sums = (mx, my, mz)

    for iteration in range(ITERS):
        final = iteration == ITERS - 1

        def second(z, carry):
            o = relax(vb, z, f[z], p[z])
            va[z + 1] = o
            gather_faces(o, z)
            return carry

        lax.fori_loop(0, depth, second, 0)
        close_faces()

        for d in range(3):
            back, ahead = face_copies(d)
            pl.when(has_prev[d])(back.start)
            pl.when(has_next[d])(ahead.start)
        if final:
            store.start()
        if iteration == 0:
            for d in range(3):
                pl.when(has_prev[d])(mortar_copy(d).wait_recv)
                h, l = split(prev[d])
                high[3 + d] = h
                low[3 + d] = l
        for d in range(3):
            back, ahead = face_copies(d)
            pl.when(has_next[d])(back.wait_recv)
            pl.when(has_prev[d])(ahead.wait_recv)

        squares = jnp.zeros((8, width), F32)
        for d in range(3):
            if d < 2:
                first, last, beyond, before = layer[2 * d], layer[2 * d + 1], near_next[d], near_prev[d]
            else:
                first, last, beyond, before = va[1], va[depth], znext[...], zprev[...]
            jump = jnp.where(has_next[d], last - dot3(beyond, high[d], low[d], NN), F32(0))
            lower = jnp.where(has_prev[d], before - dot3(first, high[3 + d], low[3 + d], NN), F32(0))
            jumps[d][...] = jump
            backs[d][...] = -dot3(lower, high[3 + d], low[3 + d], NT)
            squares = squares + tiles(jump * jump)

        line[...] = zero
        line[pl.ds(0, depth, stride=2), :] = jy[...]
        line[pl.ds(1, depth, stride=2), :] = by[...]
        spread = line[...].T
        edge = first_lane | last_lane

        def lift(z, carry, extra=None):
            o = jnp.where(edge, pltpu.roll(spread, width - 1 - 2 * z, 1), F32(0))
            top = o[:8] + jnp.where(row8 == 0, bx[pl.ds(z, 1), :], F32(0))
            end = o[-8:] + jnp.where(row8 == 7, jx[pl.ds(z, 1), :], F32(0))
            o = jnp.concatenate([top, o[8:-8], end], 0)
            if extra is not None:
                o = o + extra
            lifted[z] = o
            return carry + tiles(o * o * p[z])

        energy = lift(0, jnp.zeros((8, width), F32), bz[...])
        energy = lax.fori_loop(1, depth - 1, lift, energy)
        energy = lift(depth - 1, energy, jz[...])

        row[iteration, 0:1, :] = jnp.sum(squares, 0, keepdims=True)
        row[iteration, 1:2, :] = jnp.sum(energy, 0, keepdims=True) * (1 / DAMPING_WEIGHT)

        def tell(j, carry):
            pltpu.make_async_remote_copy(
                src_ref=row.at[iteration], dst_ref=total.at[iteration, j - 1],
                send_sem=sum_send.at[iteration], recv_sem=sum_recv.at[iteration],
                device_id=peer(j), device_id_type=MESH).start()
            return carry

        lax.fori_loop(1, n, tell, 0)
        pltpu.make_async_copy(total.at[iteration], total.at[iteration], sum_recv.at[iteration]).wait()
        pltpu.make_async_copy(total.at[iteration], total.at[iteration], sum_send.at[iteration]).wait()
        for d in range(3):
            back, ahead = face_copies(d)
            pl.when(has_prev[d])(back.wait_send)
            pl.when(has_next[d])(ahead.wait_send)
        both = jnp.sum(jnp.sum(total[iteration], 0) + row[iteration], 1, keepdims=True)
        alpha = jnp.broadcast_to(both[0:1] / (both[1:2] + EPSILON), (1, width))
        for d in range(3):
            more = alpha * jumps[d][...]
            sums[d][...] = more if iteration == 0 else sums[d][...] + more

        if not final:
            def opening(z, carry):
                supply = f[z] - alpha * lifted[z]
                f[z] = supply
                vb[z + 1] = relax(va, z, supply, p[z])
                return carry

            lax.fori_loop(0, depth, opening, 0)

    store.wait()
    for d in range(3):
        pl.when(has_next[d])(mortar_copy(d).wait_send)


def body(sizes, heat_source, conductance, projection, segment_map):
    depth, width = heat_source.shape[0], heat_source.shape[1]
    n = sizes[0] * sizes[1] * sizes[2]
    plane = (width, width)
    side = (depth, width)
    vmem = pl.BlockSpec(memory_space=pltpu.VMEM)
    anywhere = pl.BlockSpec(memory_space=pl.ANY)
    field = pltpu.VMEM((depth,) + plane, F32)
    padded = pltpu.VMEM((depth + 2,) + plane, F32)
    dma = pltpu.SemaphoreType.DMA
    state, mx, my, mz = pl.pallas_call(
        functools.partial(kernel, sizes, depth, width),
        out_shape=(
            jax.ShapeDtypeStruct(heat_source.shape, F32),
            jax.ShapeDtypeStruct(side, F32),
            jax.ShapeDtypeStruct(side, F32),
            jax.ShapeDtypeStruct(plane, F32),
        ),
        in_specs=[anywhere, anywhere, vmem, vmem],
        out_specs=(anywhere, vmem, vmem, vmem),
        scratch_shapes=[
            field, field, padded, padded, field,
            pltpu.VMEM(plane, F32), pltpu.VMEM(plane, F32),
            pltpu.VMEM((4,) + side, F32), pltpu.VMEM((2,) + side, F32), pltpu.VMEM((2,) + side, F32),
            pltpu.VMEM(plane, F32), pltpu.VMEM(plane, F32),
            pltpu.VMEM((3,) + plane, F32), pltpu.VMEM((3,) + plane, F32),
            pltpu.VMEM((6,) + plane, BF16), pltpu.VMEM((6,) + plane, BF16),
            pltpu.VMEM(side, F32), pltpu.VMEM(side, F32), pltpu.VMEM(plane, F32),
            pltpu.VMEM(side, F32), pltpu.VMEM(side, F32), pltpu.VMEM(plane, F32),
            pltpu.VMEM((ITERS, 2, width), F32), pltpu.VMEM((ITERS, n - 1, 2, width), F32),
            dma((8,)), dma, dma((6,)), dma((6,)), dma((3,)), dma((3,)), dma((ITERS,)), dma((ITERS,)),
        ],
        compiler_params=pltpu.CompilerParams(collective_id=0, has_side_effects=True),
    )(heat_source, conductance, projection[0, 0, 0], segment_map[0, 0, 0])
    return state, mx[None, None, None], my[None, None, None], mz[None, None, None]


def solution(mesh):
    in_specs = (
        P("gz", "gx", "gy"),
        P("gz", "gx", "gy"),
        P("gz", "gx", "gy", None, None, None),
        P("gz", "gx", "gy", None, None),
    )
    out_specs = (
        P("gz", "gx", "gy"),
        P("gz", "gx", "gy", None, None),
        P("gz", "gx", "gy", None, None),
        P("gz", "gx", "gy", None, None),
    )
    sizes = tuple(mesh.shape[a] for a in AXES)
    return jax.shard_map(functools.partial(body, sizes), mesh=mesh, in_specs=in_specs, out_specs=out_specs, check_vma=False)
```

```python
import functools

import jax
import jax.numpy as jnp
from jax import lax
from jax.experimental import pallas as pl
from jax.experimental.pallas import tpu as pltpu
from jax.sharding import PartitionSpec as P

ITERS = 4
SWEEPS = 2
DAMPING_WEIGHT = 0.8
EPSILON = 1e-06
GAP = 8
UNROLL = 3
LIFTS = 6
AXES = ("gx", "gy", "gz")
F32 = jnp.float32
BF16 = jnp.bfloat16
MESH = pl.DeviceIdType.MESH
NN = (((1,), (0,)), ((), ()))
NT = (((1,), (1,)), ((), ()))


def split(a):
    high = a.astype(BF16)
    return high, (a - high.astype(F32)).astype(BF16)


def dot3(a, high, low, dims):
    ah, al = split(a)
    mul = functools.partial(lax.dot_general, dimension_numbers=dims, preferred_element_type=F32)
    return mul(ah, high) + (mul(ah, low) + mul(al, high))


def tiles(a):
    return a.reshape(-1, 8, a.shape[-1]).sum(0)


def kernel(sizes, depth, width, heat, cond, proj, seg, out, mx, my, mz,
           f, p, va, vb, lifted, line, cols, layer, near_next, near_prev, znext, zprev,
           own, prev, high, low, jx, jy, jz, bx, by, bz, row, total,
           load_sem, face_send, face_recv, mortar_send, mortar_recv, sum_send, sum_recv):
    n = sizes[0] * sizes[1] * sizes[2]
    me = [lax.axis_index(a) for a in AXES]
    rank = (me[0] * sizes[1] + me[1]) * sizes[2] + me[2]
    has_next = [me[d] < sizes[d] - 1 for d in range(3)]
    has_prev = [me[d] > 0 for d in range(3)]

    def peer(j):
        t = lax.rem(rank + j, n)
        return (t // (sizes[1] * sizes[2]), lax.rem(t // sizes[2], sizes[1]), lax.rem(t, sizes[2]))

    chunks = 4
    step = depth // chunks
    loads = []
    for c in range(chunks):
        part = pl.ds(c * step, step)
        for i, (src, dst) in enumerate(((heat, f), (cond, p))):
            copy = pltpu.make_async_copy(src.at[part], dst.at[part], load_sem.at[2 * c + i])
            copy.start()
            loads.append(copy)

    barrier = pltpu.get_barrier_semaphore()

    def greet(j, carry):
        pl.semaphore_signal(barrier, inc=1, device_id=peer(j), device_id_type=MESH)
        return carry

    lax.fori_loop(1, n, greet, 0)

    rows = lax.broadcasted_iota(jnp.int32, (width, width), 0)
    lanes = lax.broadcasted_iota(jnp.int32, (width, width), 1)
    for d in range(3):
        pick = jnp.where(seg[d] == rows, F32(1), F32(0)).astype(BF16)
        ph, plow = split(proj[d])
        mh = lax.dot_general(pick, ph, NT, preferred_element_type=F32)
        ml = lax.dot_general(pick, plow, NT, preferred_element_type=F32)
        own[d] = mh + ml
        high[d] = mh.astype(BF16)
        low[d] = ml.astype(BF16)

    zero = jnp.zeros((width, width), F32)
    pitch = width + GAP
    gap = jnp.zeros((GAP, width), F32)
    for v in (va, vb):
        v[0:pitch] = jnp.zeros((pitch, width), F32)
        v[(depth + 1) * pitch:] = jnp.zeros((pitch, width), F32)

        def clear(z, carry):
            v[pl.ds(pl.multiple_of((z + 1) * pitch + width, 8), GAP), :] = gap
            return carry

        lax.fori_loop(0, depth, clear, 0)
    cols[...] = zero

    for d in range(3):
        @pl.when(jnp.logical_not(has_next[d]))
        def _():
            if d < 2:
                near_next[d] = jnp.zeros((depth, width), F32)
            else:
                znext[...] = zero

        @pl.when(jnp.logical_not(has_prev[d]))
        def _():
            prev[d] = zero
            if d < 2:
                near_prev[d] = jnp.zeros((depth, width), F32)
            else:
                zprev[...] = zero

    pl.semaphore_wait(barrier, n - 1)

    def mortar_copy(d):
        return pltpu.make_async_remote_copy(
            src_ref=own.at[d], dst_ref=prev.at[d], send_sem=mortar_send.at[d], recv_sem=mortar_recv.at[d],
            device_id={AXES[d]: me[d] + 1}, device_id_type=MESH)

    for d in range(3):
        @pl.when(has_next[d])
        def _():
            mortar_copy(d).start()

    row8 = lax.broadcasted_iota(jnp.int32, (8, width), 0)
    first_lane = lanes == 0
    last_lane = lanes == width - 1

    def shift_lanes(c):
        return (jnp.where(first_lane, F32(0), pltpu.roll(c, 1, 1))
                + jnp.where(last_lane, F32(0), pltpu.roll(c, width - 1, 1)))

    def span(z):
        return pl.ds(pl.multiple_of(z * pitch, 8), width)

    def plane(v, z):
        return v[span(z), :]

    def relax(v, z, supply, scale):
        at = (z + 1) * pitch
        c = plane(v, z + 1)
        nearby = plane(v, z) + plane(v, z + 2)
        nearby = nearby + v[pl.ds(at - 1, width), :] + v[pl.ds(at + 1, width), :]
        nearby = nearby + shift_lanes(c)
        return (1 - DAMPING_WEIGHT) * c + scale * (supply + nearby)

    def gather_faces(o, z):
        layer[0, pl.ds(z, 1), :] = o[0:1]
        layer[1, pl.ds(z, 1), :] = o[width - 1:width]
        cols[...] = jnp.where(lanes // 2 == z, pltpu.roll(o, 2 * z + 1, 1), cols[...])

    def close_faces():
        line[...] = cols[...].T
        layer[2] = line[pl.ds(1, depth, stride=2), :]
        layer[3] = line[pl.ds(0, depth, stride=2), :]

    for c in range(chunks):
        loads[2 * c].wait()
        loads[2 * c + 1].wait()

        def begin(z, carry):
            scale = DAMPING_WEIGHT / (6.0 + p[z])
            p[z] = scale
            vb[span(z + 1), :] = scale * f[z]
            return carry

        lax.fori_loop(c * step, (c + 1) * step, begin, 0, unroll=4)

    def face_copies(d):
        if d < 2:
            first, last, to_prev, to_next = layer.at[2 * d], layer.at[2 * d + 1], near_next.at[d], near_prev.at[d]
        else:
            first, last, to_prev, to_next = va.at[span(1)], va.at[span(depth)], znext, zprev
        back = pltpu.make_async_remote_copy(
            src_ref=first, dst_ref=to_prev, send_sem=face_send.at[2 * d], recv_sem=face_recv.at[2 * d],
            device_id={AXES[d]: me[d] - 1}, device_id_type=MESH)
        ahead = pltpu.make_async_remote_copy(
            src_ref=last, dst_ref=to_next, send_sem=face_send.at[2 * d + 1], recv_sem=face_recv.at[2 * d + 1],
            device_id={AXES[d]: me[d] + 1}, device_id_type=MESH)
        return back, ahead

    jumps = (jx, jy, jz)
    backs = (bx, by, bz)
    sums = (mx, my, mz)

    for iteration in range(ITERS):
        final = iteration == ITERS - 1

        def second(z, carry):
            o = relax(vb, z, f[z], p[z])
            va[span(z + 1), :] = o
            if final:
                out[z] = o
            gather_faces(o, z)
            return carry

        second(0, 0)
        second(depth - 1, 0)
        back, ahead = face_copies(2)
        pl.when(has_prev[2])(back.start)
        pl.when(has_next[2])(ahead.start)
        lax.fori_loop(1, depth - 1, second, 0, unroll=UNROLL)
        close_faces()

        for d in range(2):
            back, ahead = face_copies(d)
            pl.when(has_prev[d])(back.start)
            pl.when(has_next[d])(ahead.start)
        if iteration == 0:
            for d in range(3):
                pl.when(has_prev[d])(mortar_copy(d).wait_recv)
                h, l = split(prev[d])
                high[3 + d] = h
                low[3 + d] = l
        for d in range(3):
            back, ahead = face_copies(d)
            pl.when(has_next[d])(back.wait_recv)
            pl.when(has_prev[d])(ahead.wait_recv)

        squares = jnp.zeros((8, width), F32)
        for d in range(3):
            if d < 2:
                first, last, beyond, before = layer[2 * d], layer[2 * d + 1], near_next[d], near_prev[d]
            else:
                first, last, beyond, before = plane(va, 1), plane(va, depth), znext[...], zprev[...]
            jump = jnp.where(has_next[d], last - dot3(beyond, high[d], low[d], NN), F32(0))
            lower = jnp.where(has_prev[d], before - dot3(first, high[3 + d], low[3 + d], NN), F32(0))
            jumps[d][...] = jump
            backs[d][...] = -dot3(lower, high[3 + d], low[3 + d], NT)
            squares = squares + tiles(jump * jump)

        line[...] = zero
        line[pl.ds(0, depth, stride=2), :] = jy[...]
        line[pl.ds(1, depth, stride=2), :] = by[...]
        spread = line[...].T
        edge = first_lane | last_lane

        def lift(z, carry, extra=None):
            o = jnp.where(edge, pltpu.roll(spread, width - 1 - 2 * z, 1), F32(0))
            top = o[:8] + jnp.where(row8 == 0, bx[pl.ds(z, 1), :], F32(0))
            end = o[-8:] + jnp.where(row8 == 7, jx[pl.ds(z, 1), :], F32(0))
            o = jnp.concatenate([top, o[8:-8], end], 0)
            if extra is not None:
                o = o + extra
            lifted[z] = o
            return carry + tiles(o * o * p[z])

        energy = lift(0, jnp.zeros((8, width), F32), bz[...])
        energy = lax.fori_loop(1, depth - 1, lift, energy, unroll=LIFTS)
        energy = lift(depth - 1, energy, jz[...])

        row[iteration, 0:1, :] = jnp.sum(squares, 0, keepdims=True)
        row[iteration, 1:2, :] = jnp.sum(energy, 0, keepdims=True) * (1 / DAMPING_WEIGHT)

        def tell(j, carry):
            pltpu.make_async_remote_copy(
                src_ref=row.at[iteration], dst_ref=total.at[iteration, j - 1],
                send_sem=sum_send.at[iteration], recv_sem=sum_recv.at[iteration],
                device_id=peer(j), device_id_type=MESH).start()
            return carry

        lax.fori_loop(1, n, tell, 0)
        pltpu.make_async_copy(total.at[iteration], total.at[iteration], sum_recv.at[iteration]).wait()
        pltpu.make_async_copy(total.at[iteration], total.at[iteration], sum_send.at[iteration]).wait()
        for d in range(3):
            back, ahead = face_copies(d)
            pl.when(has_prev[d])(back.wait_send)
            pl.when(has_next[d])(ahead.wait_send)
        both = jnp.sum(jnp.sum(total[iteration], 0) + row[iteration], 1, keepdims=True)
        alpha = jnp.broadcast_to(both[0:1] / (both[1:2] + EPSILON), (1, width))
        for d in range(3):
            more = alpha * jumps[d][...]
            sums[d][...] = more if iteration == 0 else sums[d][...] + more

        if not final:
            def opening(z, carry):
                supply = f[z] - alpha * lifted[z]
                f[z] = supply
                vb[span(z + 1), :] = relax(va, z, supply, p[z])
                return carry

            lax.fori_loop(0, depth, opening, 0, unroll=4)

    for d in range(3):
        pl.when(has_next[d])(mortar_copy(d).wait_send)


def body(sizes, heat_source, conductance, projection, segment_map):
    depth, width = heat_source.shape[0], heat_source.shape[1]
    n = sizes[0] * sizes[1] * sizes[2]
    plane = (width, width)
    side = (depth, width)
    vmem = pl.BlockSpec(memory_space=pltpu.VMEM)
    anywhere = pl.BlockSpec(memory_space=pl.ANY)
    field = pltpu.VMEM((depth,) + plane, F32)
    padded = pltpu.VMEM(((depth + 2) * (width + GAP), width), F32)
    dma = pltpu.SemaphoreType.DMA
    state, mx, my, mz = pl.pallas_call(
        functools.partial(kernel, sizes, depth, width),
        out_shape=(
            pltpu.VMEM(heat_source.shape, F32),
            pltpu.VMEM(side, F32),
            pltpu.VMEM(side, F32),
            pltpu.VMEM(plane, F32),
        ),
        in_specs=[anywhere, anywhere, vmem, vmem],
        out_specs=(vmem, vmem, vmem, vmem),
        scratch_shapes=[
            field, field, padded, padded, field,
            pltpu.VMEM(plane, F32), pltpu.VMEM(plane, F32),
            pltpu.VMEM((4,) + side, F32), pltpu.VMEM((2,) + side, F32), pltpu.VMEM((2,) + side, F32),
            pltpu.VMEM(plane, F32), pltpu.VMEM(plane, F32),
            pltpu.VMEM((3,) + plane, F32), pltpu.VMEM((3,) + plane, F32),
            pltpu.VMEM((6,) + plane, BF16), pltpu.VMEM((6,) + plane, BF16),
            pltpu.VMEM(side, F32), pltpu.VMEM(side, F32), pltpu.VMEM(plane, F32),
            pltpu.VMEM(side, F32), pltpu.VMEM(side, F32), pltpu.VMEM(plane, F32),
            pltpu.VMEM((ITERS, 2, width), F32), pltpu.VMEM((ITERS, n - 1, 2, width), F32),
            dma((8,)), dma((6,)), dma((6,)), dma((3,)), dma((3,)), dma((ITERS,)), dma((ITERS,)),
        ],
        compiler_params=pltpu.CompilerParams(collective_id=0, has_side_effects=True),
    )(heat_source, conductance, projection[0, 0, 0], jnp.swapaxes(segment_map[0, 0], 0, 1))
    return state, mx[None, None, None], my[None, None, None], mz[None, None, None]


def solution(mesh):
    in_specs = (
        P("gz", "gx", "gy"),
        P("gz", "gx", "gy"),
        P("gz", "gx", "gy", None, None, None),
        P("gz", "gx", "gy", None, None),
    )
    out_specs = (
        P("gz", "gx", "gy"),
        P("gz", "gx", "gy", None, None),
        P("gz", "gx", "gy", None, None),
        P("gz", "gx", "gy", None, None),
    )
    sizes = tuple(mesh.shape[a] for a in AXES)
    return jax.shard_map(functools.partial(body, sizes), mesh=mesh, in_specs=in_specs, out_specs=out_specs, check_vma=False)
```

```python
import functools

import jax
import jax.numpy as jnp
from jax import lax
from jax.experimental import pallas as pl
from jax.experimental.pallas import tpu as pltpu
from jax.sharding import PartitionSpec as P

ITERS = 4
SWEEPS = 2
DAMPING_WEIGHT = 0.8
EPSILON = 1e-06
GAP = 8
UNROLL = 3
LIFTS = 6
AXES = ("gx", "gy", "gz")
F32 = jnp.float32
BF16 = jnp.bfloat16
MESH = pl.DeviceIdType.MESH
NN = (((1,), (0,)), ((), ()))
NT = (((1,), (1,)), ((), ()))


def split(a):
    high = a.astype(BF16)
    return high, (a - high.astype(F32)).astype(BF16)


def dot3(a, high, low, dims):
    ah, al = split(a)
    mul = functools.partial(lax.dot_general, dimension_numbers=dims, preferred_element_type=F32)
    return mul(ah, high) + (mul(ah, low) + mul(al, high))


def tiles(a):
    return a.reshape(-1, 8, a.shape[-1]).sum(0)


def kernel(sizes, depth, width, heat, cond, proj, seg, out, mx, my, mz,
           f, p, va, vb, lifted, push, line, cols, layer, rim, near_next, near_prev, znext, zprev,
           own, prev, high, low, jx, jy, jz, bx, by, bz, row, total,
           load_sem, face_send, face_recv, mortar_send, mortar_recv, sum_send, sum_recv):
    n = sizes[0] * sizes[1] * sizes[2]
    me = [lax.axis_index(a) for a in AXES]
    rank = (me[0] * sizes[1] + me[1]) * sizes[2] + me[2]
    has_next = [me[d] < sizes[d] - 1 for d in range(3)]
    has_prev = [me[d] > 0 for d in range(3)]

    def peer(j):
        t = lax.rem(rank + j, n)
        return (t // (sizes[1] * sizes[2]), lax.rem(t // sizes[2], sizes[1]), lax.rem(t, sizes[2]))

    chunks = 4
    step = depth // chunks
    loads = []
    for c in range(chunks):
        part = pl.ds(c * step, step)
        for i, (src, dst) in enumerate(((heat, f), (cond, p))):
            copy = pltpu.make_async_copy(src.at[part], dst.at[part], load_sem.at[2 * c + i])
            copy.start()
            loads.append(copy)

    barrier = pltpu.get_barrier_semaphore()

    def greet(j, carry):
        pl.semaphore_signal(barrier, inc=1, device_id=peer(j), device_id_type=MESH)
        return carry

    lax.fori_loop(1, n, greet, 0)

    rows = lax.broadcasted_iota(jnp.int32, (width, width), 0)
    lanes = lax.broadcasted_iota(jnp.int32, (width, width), 1)
    for d in range(3):
        pick = jnp.where(seg[d] == rows, F32(1), F32(0)).astype(BF16)
        ph, plow = split(proj[d])
        mh = lax.dot_general(pick, ph, NT, preferred_element_type=F32)
        ml = lax.dot_general(pick, plow, NT, preferred_element_type=F32)
        own[d] = mh + ml
        high[d] = mh.astype(BF16)
        low[d] = ml.astype(BF16)

    zero = jnp.zeros((width, width), F32)
    pitch = width + GAP
    gap = jnp.zeros((GAP, width), F32)
    for v in (va, vb):
        v[0:pitch] = jnp.zeros((pitch, width), F32)
        v[(depth + 1) * pitch:] = jnp.zeros((pitch, width), F32)

        def clear(z, carry):
            v[pl.ds(pl.multiple_of((z + 1) * pitch + width, 8), GAP), :] = gap
            return carry

        lax.fori_loop(0, depth, clear, 0)
    cols[...] = zero

    for d in range(3):
        @pl.when(jnp.logical_not(has_next[d]))
        def _():
            if d < 2:
                near_next[d] = jnp.zeros((depth, width), F32)
            else:
                znext[...] = zero

        @pl.when(jnp.logical_not(has_prev[d]))
        def _():
            prev[d] = zero
            if d < 2:
                near_prev[d] = jnp.zeros((depth, width), F32)
            else:
                zprev[...] = zero

    row8 = lax.broadcasted_iota(jnp.int32, (8, width), 0)
    srow = lax.broadcasted_iota(jnp.int32, (depth, width), 0)
    slane = lax.broadcasted_iota(jnp.int32, (depth, width), 1)
    sedge = (slane == 0) | (slane == width - 1)
    inner = (rows > 0) & (rows < width - 1) & (lanes > 0) & (lanes < width - 1)
    first_lane = lanes == 0
    last_lane = lanes == width - 1

    def shift_lanes(c):
        return (jnp.where(first_lane, F32(0), pltpu.roll(c, 1, 1))
                + jnp.where(last_lane, F32(0), pltpu.roll(c, width - 1, 1)))

    def span(z):
        return pl.ds(pl.multiple_of(z * pitch, 8), width)

    def plane(v, z):
        return v[span(z), :]

    def relax(v, z, supply, scale):
        at = (z + 1) * pitch
        c = plane(v, z + 1)
        nearby = plane(v, z) + plane(v, z + 2)
        nearby = nearby + v[pl.ds(at - 1, width), :] + v[pl.ds(at + 1, width), :]
        nearby = nearby + shift_lanes(c)
        return (1 - DAMPING_WEIGHT) * c + scale * (supply + nearby)

    def gather_faces(o, z):
        layer[0, pl.ds(z, 1), :] = o[0:1]
        layer[1, pl.ds(z, 1), :] = o[width - 1:width]
        cols[...] = jnp.where(lanes // 2 == z, pltpu.roll(o, 2 * z + 1, 1), cols[...])

    def close_faces(into):
        line[...] = cols[...].T
        into[2] = line[pl.ds(1, depth, stride=2), :]
        into[3] = line[pl.ds(0, depth, stride=2), :]

    for c in range(chunks):
        loads[2 * c].wait()
        loads[2 * c + 1].wait()

        def begin(z, carry):
            scale = DAMPING_WEIGHT / (6.0 + p[z])
            p[z] = scale
            rim[0, pl.ds(z, 1), :] = scale[0:1]
            rim[1, pl.ds(z, 1), :] = scale[width - 1:width]
            cols[...] = jnp.where(lanes // 2 == z, pltpu.roll(scale, 2 * z + 1, 1), cols[...])
            vb[span(z + 1), :] = scale * f[z]
            return carry

        lax.fori_loop(c * step, (c + 1) * step, begin, 0, unroll=4)

    close_faces(rim)
    pl.semaphore_wait(barrier, n - 1)

    def mortar_copy(d):
        return pltpu.make_async_remote_copy(
            src_ref=own.at[d], dst_ref=prev.at[d], send_sem=mortar_send.at[d], recv_sem=mortar_recv.at[d],
            device_id={AXES[d]: me[d] + 1}, device_id_type=MESH)

    for d in range(3):
        @pl.when(has_next[d])
        def _():
            mortar_copy(d).start()

    def face_copies(d):
        if d < 2:
            first, last, to_prev, to_next = layer.at[2 * d], layer.at[2 * d + 1], near_next.at[d], near_prev.at[d]
        else:
            first, last, to_prev, to_next = va.at[span(1)], va.at[span(depth)], znext, zprev
        back = pltpu.make_async_remote_copy(
            src_ref=first, dst_ref=to_prev, send_sem=face_send.at[2 * d], recv_sem=face_recv.at[2 * d],
            device_id={AXES[d]: me[d] - 1}, device_id_type=MESH)
        ahead = pltpu.make_async_remote_copy(
            src_ref=last, dst_ref=to_next, send_sem=face_send.at[2 * d + 1], recv_sem=face_recv.at[2 * d + 1],
            device_id={AXES[d]: me[d] + 1}, device_id_type=MESH)
        return back, ahead

    jumps = (jx, jy, jz)
    backs = (bx, by, bz)
    sums = (mx, my, mz)

    for iteration in range(ITERS):
        final = iteration == ITERS - 1

        def second(z, carry):
            o = relax(vb, z, f[z], p[z])
            va[span(z + 1), :] = o
            if final:
                out[z] = o
            gather_faces(o, z)
            return carry

        second(0, 0)
        second(depth - 1, 0)
        back, ahead = face_copies(2)
        pl.when(has_prev[2])(back.start)
        pl.when(has_next[2])(ahead.start)
        lax.fori_loop(1, depth - 1, second, 0, unroll=UNROLL)
        close_faces(layer)

        for d in range(2):
            back, ahead = face_copies(d)
            pl.when(has_prev[d])(back.start)
            pl.when(has_next[d])(ahead.start)
        if iteration == 0:
            for d in range(3):
                pl.when(has_prev[d])(mortar_copy(d).wait_recv)
                h, l = split(prev[d])
                high[3 + d] = h
                low[3 + d] = l
        sent = []
        for d in range(3):
            first = layer[2 * d] if d < 2 else plane(va, 1)
            sent.append(dot3(first, high[3 + d], low[3 + d], NN))
        for d in range(3):
            back, ahead = face_copies(d)
            pl.when(has_next[d])(back.wait_recv)
            pl.when(has_prev[d])(ahead.wait_recv)

        squares = jnp.zeros((8, width), F32)
        for d in range(3):
            if d < 2:
                last, beyond, before = layer[2 * d + 1], near_next[d], near_prev[d]
            else:
                last, beyond, before = plane(va, depth), znext[...], zprev[...]
            jump = jnp.where(has_next[d], last - dot3(beyond, high[d], low[d], NN), F32(0))
            lower = jnp.where(has_prev[d], before - sent[d], F32(0))
            jumps[d][...] = jump
            backs[d][...] = -dot3(lower, high[3 + d], low[3 + d], NT)
            squares = squares + tiles(jump * jump)

        gx, gy, gz, hx, hy, hz = jx[...], jy[...], jz[...], bx[...], by[...], bz[...]
        gzt, hzt = gz.T, hz.T

        def ends(a, bottom, top):
            return a + jnp.where(srow == 0, bottom, F32(0)) + jnp.where(srow == depth - 1, top, F32(0))

        def sides(a, left, right):
            return a + jnp.where(slane == 0, left, F32(0)) + jnp.where(slane == width - 1, right, F32(0))

        y0 = ends(sides(hy, hx, pltpu.roll(gx, width - 1, 1)), hzt[:1], gzt[:1])
        y1 = ends(sides(gy, pltpu.roll(hx, 1, 1), gx), hzt[width - 1:], gzt[width - 1:])
        x0 = jnp.where(sedge, F32(0), ends(hx, hz[:1], gz[:1]))
        x1 = jnp.where(sedge, F32(0), ends(gx, hz[width - 1:], gz[width - 1:]))
        z0 = jnp.where(inner, hz, F32(0))
        z1 = jnp.where(inner, gz, F32(0))
        energy = (tiles(y0 * y0 * rim[2]) + tiles(y1 * y1 * rim[3])
                  + tiles(x0 * x0 * rim[0]) + tiles(x1 * x1 * rim[1])
                  + tiles(z0 * z0 * p[0]) + tiles(z1 * z1 * p[depth - 1]))

        row[iteration, 0:1, :] = jnp.sum(squares, 0, keepdims=True)
        row[iteration, 1:2, :] = jnp.sum(energy, 0, keepdims=True) * (1 / DAMPING_WEIGHT)

        def tell(j, carry):
            pltpu.make_async_remote_copy(
                src_ref=row.at[iteration], dst_ref=total.at[iteration, j - 1],
                send_sem=sum_send.at[iteration], recv_sem=sum_recv.at[iteration],
                device_id=peer(j), device_id_type=MESH).start()
            return carry

        lax.fori_loop(1, n, tell, 0)
        if not final:
            line[...] = zero
            line[pl.ds(0, depth, stride=2), :] = jy[...]
            line[pl.ds(1, depth, stride=2), :] = by[...]
            spread = line[...].T
            edge = first_lane | last_lane

            def lift(z, carry, extra=None):
                o = jnp.where(edge, pltpu.roll(spread, width - 1 - 2 * z, 1), F32(0))
                top = o[:8] + jnp.where(row8 == 0, bx[pl.ds(z, 1), :], F32(0))
                end = o[-8:] + jnp.where(row8 == 7, jx[pl.ds(z, 1), :], F32(0))
                o = jnp.concatenate([top, o[8:-8], end], 0)
                if extra is not None:
                    o = o + extra
                lifted[z] = o
                push[z] = o * p[z]
                return carry

            lift(0, 0, bz[...])
            lax.fori_loop(1, depth - 1, lift, 0, unroll=LIFTS)
            lift(depth - 1, 0, jz[...])

            def opening(z, carry):
                vb[span(z + 1), :] = relax(va, z, f[z], p[z])
                return carry

            lax.fori_loop(0, depth, opening, 0, unroll=4)

        pltpu.make_async_copy(total.at[iteration], total.at[iteration], sum_recv.at[iteration]).wait()
        pltpu.make_async_copy(total.at[iteration], total.at[iteration], sum_send.at[iteration]).wait()
        for d in range(3):
            back, ahead = face_copies(d)
            pl.when(has_prev[d])(back.wait_send)
            pl.when(has_next[d])(ahead.wait_send)
        both = jnp.sum(jnp.sum(total[iteration], 0) + row[iteration], 1, keepdims=True)
        alpha = jnp.broadcast_to(both[0:1] / (both[1:2] + EPSILON), (1, width))
        for d in range(3):
            more = alpha * jumps[d][...]
            sums[d][...] = more if iteration == 0 else sums[d][...] + more

        if not final:
            def correct(z, carry):
                f[z] = f[z] - alpha * lifted[z]
                vb[span(z + 1), :] = plane(vb, z + 1) - alpha * push[z]
                return carry

            lax.fori_loop(0, depth, correct, 0, unroll=2)

    for d in range(3):
        pl.when(has_next[d])(mortar_copy(d).wait_send)


def body(sizes, heat_source, conductance, projection, segment_map):
    depth, width = heat_source.shape[0], heat_source.shape[1]
    n = sizes[0] * sizes[1] * sizes[2]
    plane = (width, width)
    side = (depth, width)
    vmem = pl.BlockSpec(memory_space=pltpu.VMEM)
    anywhere = pl.BlockSpec(memory_space=pl.ANY)
    field = pltpu.VMEM((depth,) + plane, F32)
    padded = pltpu.VMEM(((depth + 2) * (width + GAP), width), F32)
    dma = pltpu.SemaphoreType.DMA
    state, mx, my, mz = pl.pallas_call(
        functools.partial(kernel, sizes, depth, width),
        out_shape=(
            pltpu.VMEM(heat_source.shape, F32),
            pltpu.VMEM(side, F32),
            pltpu.VMEM(side, F32),
            pltpu.VMEM(plane, F32),
        ),
        in_specs=[anywhere, anywhere, vmem, vmem],
        out_specs=(vmem, vmem, vmem, vmem),
        scratch_shapes=[
            field, field, padded, padded, field, field,
            pltpu.VMEM(plane, F32), pltpu.VMEM(plane, F32),
            pltpu.VMEM((4,) + side, F32), pltpu.VMEM((4,) + side, F32), pltpu.VMEM((2,) + side, F32), pltpu.VMEM((2,) + side, F32),
            pltpu.VMEM(plane, F32), pltpu.VMEM(plane, F32),
            pltpu.VMEM((3,) + plane, F32), pltpu.VMEM((3,) + plane, F32),
            pltpu.VMEM((6,) + plane, BF16), pltpu.VMEM((6,) + plane, BF16),
            pltpu.VMEM(side, F32), pltpu.VMEM(side, F32), pltpu.VMEM(plane, F32),
            pltpu.VMEM(side, F32), pltpu.VMEM(side, F32), pltpu.VMEM(plane, F32),
            pltpu.VMEM((ITERS, 2, width), F32), pltpu.VMEM((ITERS, n - 1, 2, width), F32),
            dma((8,)), dma((6,)), dma((6,)), dma((3,)), dma((3,)), dma((ITERS,)), dma((ITERS,)),
        ],
        compiler_params=pltpu.CompilerParams(collective_id=0, has_side_effects=True),
    )(heat_source, conductance, projection[0, 0, 0], jnp.swapaxes(segment_map[0, 0], 0, 1))
    return state, mx[None, None, None], my[None, None, None], mz[None, None, None]


def solution(mesh):
    in_specs = (
        P("gz", "gx", "gy"),
        P("gz", "gx", "gy"),
        P("gz", "gx", "gy", None, None, None),
        P("gz", "gx", "gy", None, None),
    )
    out_specs = (
        P("gz", "gx", "gy"),
        P("gz", "gx", "gy", None, None),
        P("gz", "gx", "gy", None, None),
        P("gz", "gx", "gy", None, None),
    )
    sizes = tuple(mesh.shape[a] for a in AXES)
    return jax.shard_map(functools.partial(body, sizes), mesh=mesh, in_specs=in_specs, out_specs=out_specs, check_vma=False)
```

```python
import functools
import itertools

import jax
import jax.numpy as jnp
from jax import lax
from jax.experimental import pallas as pl
from jax.experimental.pallas import tpu as pltpu
from jax.sharding import PartitionSpec as P

ITERS = 4
SWEEPS = 2
DAMPING_WEIGHT = 0.8
EPSILON = 1e-06
GAP = 8
UNROLL = 3
LIFTS = 6
AXES = ("gx", "gy", "gz")
F32 = jnp.float32
BF16 = jnp.bfloat16
MESH = pl.DeviceIdType.MESH
NN = (((1,), (0,)), ((), ()))
NT = (((1,), (1,)), ((), ()))


def split(a):
    high = a.astype(BF16)
    return high, (a - high.astype(F32)).astype(BF16)


def dot3(a, high, low, dims):
    ah, al = split(a)
    mul = functools.partial(lax.dot_general, dimension_numbers=dims, preferred_element_type=F32)
    return mul(ah, high) + (mul(ah, low) + mul(al, high))


def tiles(a):
    return a.reshape(-1, 8, a.shape[-1]).sum(0)


def kernel(sizes, depth, width, heat, cond, proj, seg, out, mx, my, mz,
           f, p, va, vb, lifted, push, line, cols, layer, rim, near_next, near_prev, znext, zprev,
           own, prev, high, low, jx, jy, jz, bx, by, bz, row, total,
           load_sem, face_send, face_recv, mortar_send, mortar_recv, sum_send, sum_recv):
    n = sizes[0] * sizes[1] * sizes[2]
    me = [lax.axis_index(a) for a in AXES]
    has_next = [me[d] < sizes[d] - 1 for d in range(3)]
    has_prev = [me[d] > 0 for d in range(3)]

    def around(d):
        return [me[d]] + [jnp.where(me[d] + k >= sizes[d], me[d] + k - sizes[d], me[d] + k) for k in range(1, sizes[d])]

    peers = list(itertools.product(*(around(d) for d in range(3))))[1:]

    chunks = 4
    step = depth // chunks
    loads = []
    for c in range(chunks):
        part = pl.ds(c * step, step)
        for i, (src, dst) in enumerate(((heat, f), (cond, p))):
            copy = pltpu.make_async_copy(src.at[part], dst.at[part], load_sem.at[2 * c + i])
            copy.start()
            loads.append(copy)

    barrier = pltpu.get_barrier_semaphore()

    for peer in peers:
        pl.semaphore_signal(barrier, inc=1, device_id=peer, device_id_type=MESH)

    rows = lax.broadcasted_iota(jnp.int32, (width, width), 0)
    lanes = lax.broadcasted_iota(jnp.int32, (width, width), 1)
    for d in range(3):
        pick = jnp.where(seg[d] == rows, F32(1), F32(0)).astype(BF16)
        ph, plow = split(proj[d])
        mh = lax.dot_general(pick, ph, NT, preferred_element_type=F32)
        ml = lax.dot_general(pick, plow, NT, preferred_element_type=F32)
        own[d] = mh + ml
        high[d] = mh.astype(BF16)
        low[d] = ml.astype(BF16)

    zero = jnp.zeros((width, width), F32)
    pitch = width + GAP
    gap = jnp.zeros((GAP, width), F32)
    for v in (va, vb):
        v[0:pitch] = jnp.zeros((pitch, width), F32)
        v[(depth + 1) * pitch:] = jnp.zeros((pitch, width), F32)

        def clear(z, carry):
            v[pl.ds(pl.multiple_of((z + 1) * pitch + width, 8), GAP), :] = gap
            return carry

        lax.fori_loop(0, depth, clear, 0)
    cols[...] = zero

    for d in range(3):
        @pl.when(jnp.logical_not(has_next[d]))
        def _():
            if d < 2:
                near_next[d] = jnp.zeros((depth, width), F32)
            else:
                znext[...] = zero

        @pl.when(jnp.logical_not(has_prev[d]))
        def _():
            prev[d] = zero
            if d < 2:
                near_prev[d] = jnp.zeros((depth, width), F32)
            else:
                zprev[...] = zero

    row8 = lax.broadcasted_iota(jnp.int32, (8, width), 0)
    srow = lax.broadcasted_iota(jnp.int32, (depth, width), 0)
    slane = lax.broadcasted_iota(jnp.int32, (depth, width), 1)
    sedge = (slane == 0) | (slane == width - 1)
    inner = (rows > 0) & (rows < width - 1) & (lanes > 0) & (lanes < width - 1)
    first_lane = lanes == 0
    last_lane = lanes == width - 1

    def shift_lanes(c):
        return (jnp.where(first_lane, F32(0), pltpu.roll(c, 1, 1))
                + jnp.where(last_lane, F32(0), pltpu.roll(c, width - 1, 1)))

    def span(z):
        return pl.ds(pl.multiple_of(z * pitch, 8), width)

    def plane(v, z):
        return v[span(z), :]

    def relax(v, z, supply, scale):
        at = (z + 1) * pitch
        c = plane(v, z + 1)
        nearby = plane(v, z) + plane(v, z + 2)
        nearby = nearby + v[pl.ds(at - 1, width), :] + v[pl.ds(at + 1, width), :]
        nearby = nearby + shift_lanes(c)
        return (1 - DAMPING_WEIGHT) * c + scale * (supply + nearby)

    def gather_faces(o, z):
        layer[0, pl.ds(z, 1), :] = o[0:1]
        layer[1, pl.ds(z, 1), :] = o[width - 1:width]
        cols[...] = jnp.where(lanes // 2 == z, pltpu.roll(o, 2 * z + 1, 1), cols[...])

    def close_faces(into):
        line[...] = cols[...].T
        into[2] = line[pl.ds(1, depth, stride=2), :]
        into[3] = line[pl.ds(0, depth, stride=2), :]

    for c in range(chunks):
        loads[2 * c].wait()
        loads[2 * c + 1].wait()

        def begin(z, carry):
            scale = DAMPING_WEIGHT / (6.0 + p[z])
            p[z] = scale
            rim[0, pl.ds(z, 1), :] = scale[0:1]
            rim[1, pl.ds(z, 1), :] = scale[width - 1:width]
            cols[...] = jnp.where(lanes // 2 == z, pltpu.roll(scale, 2 * z + 1, 1), cols[...])
            vb[span(z + 1), :] = scale * f[z]
            return carry

        lax.fori_loop(c * step, (c + 1) * step, begin, 0, unroll=4)

    close_faces(rim)
    pl.semaphore_wait(barrier, n - 1)

    def mortar_copy(d):
        return pltpu.make_async_remote_copy(
            src_ref=own.at[d], dst_ref=prev.at[d], send_sem=mortar_send.at[d], recv_sem=mortar_recv.at[d],
            device_id={AXES[d]: me[d] + 1}, device_id_type=MESH)

    for d in range(3):
        @pl.when(has_next[d])
        def _():
            mortar_copy(d).start()

    def face_copies(d):
        if d < 2:
            first, last, to_prev, to_next = layer.at[2 * d], layer.at[2 * d + 1], near_next.at[d], near_prev.at[d]
        else:
            first, last, to_prev, to_next = va.at[span(1)], va.at[span(depth)], znext, zprev
        back = pltpu.make_async_remote_copy(
            src_ref=first, dst_ref=to_prev, send_sem=face_send.at[2 * d], recv_sem=face_recv.at[2 * d],
            device_id={AXES[d]: me[d] - 1}, device_id_type=MESH)
        ahead = pltpu.make_async_remote_copy(
            src_ref=last, dst_ref=to_next, send_sem=face_send.at[2 * d + 1], recv_sem=face_recv.at[2 * d + 1],
            device_id={AXES[d]: me[d] + 1}, device_id_type=MESH)
        return back, ahead

    jumps = (jx, jy, jz)
    backs = (bx, by, bz)
    sums = (mx, my, mz)

    for iteration in range(ITERS):
        final = iteration == ITERS - 1

        def second(z, carry):
            supply = f[z] if iteration == 0 else f[z] - alpha * lifted[z]
            o = relax(vb, z, supply, p[z])
            va[span(z + 1), :] = o
            if final:
                out[z] = o
            gather_faces(o, z)
            return carry

        second(0, 0)
        second(depth - 1, 0)
        back, ahead = face_copies(2)
        pl.when(has_prev[2])(back.start)
        pl.when(has_next[2])(ahead.start)
        lax.fori_loop(1, depth - 1, second, 0, unroll=UNROLL)
        close_faces(layer)

        for d in range(2):
            back, ahead = face_copies(d)
            pl.when(has_prev[d])(back.start)
            pl.when(has_next[d])(ahead.start)
        if iteration == 0:
            for d in range(3):
                pl.when(has_prev[d])(mortar_copy(d).wait_recv)
                h, l = split(prev[d])
                high[3 + d] = h
                low[3 + d] = l
        if iteration > 0 and not final:
            def settle(z, carry):
                f[z] = f[z] - alpha * lifted[z]
                return carry

            lax.fori_loop(0, depth, settle, 0, unroll=2)

        sent = []
        for d in range(3):
            first = layer[2 * d] if d < 2 else plane(va, 1)
            sent.append(dot3(first, high[3 + d], low[3 + d], NN))
        for d in range(3):
            back, ahead = face_copies(d)
            pl.when(has_next[d])(back.wait_recv)
            pl.when(has_prev[d])(ahead.wait_recv)

        squares = jnp.zeros((8, width), F32)
        for d in range(3):
            if d < 2:
                last, beyond, before = layer[2 * d + 1], near_next[d], near_prev[d]
            else:
                last, beyond, before = plane(va, depth), znext[...], zprev[...]
            jump = jnp.where(has_next[d], last - dot3(beyond, high[d], low[d], NN), F32(0))
            lower = jnp.where(has_prev[d], before - sent[d], F32(0))
            jumps[d][...] = jump
            backs[d][...] = -dot3(lower, high[3 + d], low[3 + d], NT)
            squares = squares + tiles(jump * jump)

        gx, gy, gz, hx, hy, hz = jx[...], jy[...], jz[...], bx[...], by[...], bz[...]
        gzt, hzt = gz.T, hz.T

        def ends(a, bottom, top):
            return a + jnp.where(srow == 0, bottom, F32(0)) + jnp.where(srow == depth - 1, top, F32(0))

        def sides(a, left, right):
            return a + jnp.where(slane == 0, left, F32(0)) + jnp.where(slane == width - 1, right, F32(0))

        y0 = ends(sides(hy, hx, pltpu.roll(gx, width - 1, 1)), hzt[:1], gzt[:1])
        y1 = ends(sides(gy, pltpu.roll(hx, 1, 1), gx), hzt[width - 1:], gzt[width - 1:])
        x0 = jnp.where(sedge, F32(0), ends(hx, hz[:1], gz[:1]))
        x1 = jnp.where(sedge, F32(0), ends(gx, hz[width - 1:], gz[width - 1:]))
        z0 = jnp.where(inner, hz, F32(0))
        z1 = jnp.where(inner, gz, F32(0))
        energy = (tiles(y0 * y0 * rim[2]) + tiles(y1 * y1 * rim[3])
                  + tiles(x0 * x0 * rim[0]) + tiles(x1 * x1 * rim[1])
                  + tiles(z0 * z0 * p[0]) + tiles(z1 * z1 * p[depth - 1]))

        row[iteration, 0:1, :] = jnp.sum(squares, 0, keepdims=True)
        row[iteration, 1:2, :] = jnp.sum(energy, 0, keepdims=True) * (1 / DAMPING_WEIGHT)

        for slot, peer in enumerate(peers):
            pltpu.make_async_remote_copy(
                src_ref=row.at[iteration], dst_ref=total.at[iteration, slot],
                send_sem=sum_send.at[iteration], recv_sem=sum_recv.at[iteration],
                device_id=peer, device_id_type=MESH).start()
        if not final:
            line[...] = zero
            line[pl.ds(0, depth, stride=2), :] = jy[...]
            line[pl.ds(1, depth, stride=2), :] = by[...]
            spread = line[...].T
            edge = first_lane | last_lane

            def lift(z, carry, extra=None):
                o = jnp.where(edge, pltpu.roll(spread, width - 1 - 2 * z, 1), F32(0))
                top = o[:8] + jnp.where(row8 == 0, bx[pl.ds(z, 1), :], F32(0))
                end = o[-8:] + jnp.where(row8 == 7, jx[pl.ds(z, 1), :], F32(0))
                o = jnp.concatenate([top, o[8:-8], end], 0)
                if extra is not None:
                    o = o + extra
                lifted[z] = o
                push[z] = o * p[z]
                return carry

            lift(0, 0, bz[...])
            lax.fori_loop(1, depth - 1, lift, 0, unroll=LIFTS)
            lift(depth - 1, 0, jz[...])

            def opening(z, carry):
                vb[span(z + 1), :] = relax(va, z, f[z], p[z])
                return carry

            lax.fori_loop(0, depth, opening, 0, unroll=4)

        pltpu.make_async_copy(total.at[iteration], total.at[iteration], sum_recv.at[iteration]).wait()
        pltpu.make_async_copy(total.at[iteration], total.at[iteration], sum_send.at[iteration]).wait()
        for d in range(3):
            back, ahead = face_copies(d)
            pl.when(has_prev[d])(back.wait_send)
            pl.when(has_next[d])(ahead.wait_send)
        both = jnp.sum(jnp.sum(total[iteration], 0) + row[iteration], 1, keepdims=True)
        alpha = jnp.broadcast_to(both[0:1] / (both[1:2] + EPSILON), (1, width))
        for d in range(3):
            more = alpha * jumps[d][...]
            sums[d][...] = more if iteration == 0 else sums[d][...] + more

        if not final:
            def correct(z, carry):
                vb[span(z + 1), :] = plane(vb, z + 1) - alpha * push[z]
                return carry

            lax.fori_loop(0, depth, correct, 0, unroll=2)

    for d in range(3):
        pl.when(has_next[d])(mortar_copy(d).wait_send)


def body(sizes, heat_source, conductance, projection, segment_map):
    depth, width = heat_source.shape[0], heat_source.shape[1]
    n = sizes[0] * sizes[1] * sizes[2]
    plane = (width, width)
    side = (depth, width)
    vmem = pl.BlockSpec(memory_space=pltpu.VMEM)
    anywhere = pl.BlockSpec(memory_space=pl.ANY)
    field = pltpu.VMEM((depth,) + plane, F32)
    padded = pltpu.VMEM(((depth + 2) * (width + GAP), width), F32)
    dma = pltpu.SemaphoreType.DMA
    state, mx, my, mz = pl.pallas_call(
        functools.partial(kernel, sizes, depth, width),
        out_shape=(
            pltpu.VMEM(heat_source.shape, F32),
            pltpu.VMEM(side, F32),
            pltpu.VMEM(side, F32),
            pltpu.VMEM(plane, F32),
        ),
        in_specs=[anywhere, anywhere, vmem, vmem],
        out_specs=(vmem, vmem, vmem, vmem),
        scratch_shapes=[
            field, field, padded, padded, field, field,
            pltpu.VMEM(plane, F32), pltpu.VMEM(plane, F32),
            pltpu.VMEM((4,) + side, F32), pltpu.VMEM((4,) + side, F32), pltpu.VMEM((2,) + side, F32), pltpu.VMEM((2,) + side, F32),
            pltpu.VMEM(plane, F32), pltpu.VMEM(plane, F32),
            pltpu.VMEM((3,) + plane, F32), pltpu.VMEM((3,) + plane, F32),
            pltpu.VMEM((6,) + plane, BF16), pltpu.VMEM((6,) + plane, BF16),
            pltpu.VMEM(side, F32), pltpu.VMEM(side, F32), pltpu.VMEM(plane, F32),
            pltpu.VMEM(side, F32), pltpu.VMEM(side, F32), pltpu.VMEM(plane, F32),
            pltpu.VMEM((ITERS, 2, width), F32), pltpu.VMEM((ITERS, n - 1, 2, width), F32),
            dma((8,)), dma((6,)), dma((6,)), dma((3,)), dma((3,)), dma((ITERS,)), dma((ITERS,)),
        ],
        compiler_params=pltpu.CompilerParams(collective_id=0, has_side_effects=True),
    )(heat_source, conductance, projection[0, 0, 0], jnp.swapaxes(segment_map[0, 0], 0, 1))
    return state, mx[None, None, None], my[None, None, None], mz[None, None, None]


def solution(mesh):
    in_specs = (
        P("gz", "gx", "gy"),
        P("gz", "gx", "gy"),
        P("gz", "gx", "gy", None, None, None),
        P("gz", "gx", "gy", None, None),
    )
    out_specs = (
        P("gz", "gx", "gy"),
        P("gz", "gx", "gy", None, None),
        P("gz", "gx", "gy", None, None),
        P("gz", "gx", "gy", None, None),
    )
    sizes = tuple(mesh.shape[a] for a in AXES)
    return jax.shard_map(functools.partial(body, sizes), mesh=mesh, in_specs=in_specs, out_specs=out_specs, check_vma=False)
```
